32 devices in a mesh: rep: 8 (over y, x, core), zero: 4 (over z).
Axes of the slice: x: 2, y: 2, z: 4, core: 2. Of those that a mesh axis runs over, the one named last changes fastest.
Arguments:
- grads: bfloat16 [8, 4, 4194304], P('rep', 'zero'), may hold values from -6 to 6
- master: float32 [8, 4194304], P('rep', 'zero'), may hold values from -6 to 6
- moment_one: float32 [8, 4194304], P('rep', 'zero'), may hold values from -0.4375 to 0.4375
- moment_two: float32 [8, 4194304], P('rep', 'zero'), may hold values from 0.0001 to 0.01
- step_index: int32 [1], replicated, may hold values from 0 to 999
Outputs:
- master_out: float32 [8, 4194304], P('rep', 'zero')
- moment_one_out: float32 [8, 4194304], P('rep', 'zero')
- moment_two_out: float32 [8, 4194304], P('rep', 'zero')
- params_out: bfloat16 [8, 4194304], P('rep')
The draws below stay inside these ranges and needn't reach their ends.
All inputs are finite; a program needn't handle non-finite values.
Results may differ from the reference program's by a relative error of at most 0.0075.
Values may be sent and summed in bfloat16 or wider, within the bound.
No kernel may reach another device: no remote copies, remote signals or barrier semaphores. Data moves between devices by JAX's collectives and lax.ppermute only.
A program may use at most 192 MiB of HBM per device.

```python
import math
import jax
import jax.numpy as jnp

P_SIZE = 4194304
REPS = 8
LOOP = 4
N_REP = 8
N_ZERO = 4


def block_levels(stream_key, shape, cuts, smallest, high):
    def one(dim, parts):
        draws = jax.random.uniform(jax.random.fold_in(jax.random.fold_in(stream_key, 6), dim), (parts,), jnp.float32, smallest / len(cuts), high / len(cuts))
        return jnp.repeat(jnp.exp(draws), shape[dim] // parts).reshape((-1,) + (1,) * (len(shape) - dim - 1))

    factor_of = one(*cuts[0])
    for cut in cuts[1:]:
        factor_of = factor_of * one(*cut)
    return factor_of


def scatter_about(own_key, shape, scale, reach, shards=(), kind=jnp.bfloat16):
    values = scale * jax.random.normal(own_key, shape, jnp.float32)
    if shards:
        values = values * block_levels(own_key, shape, shards, -0.22, 0.18)
    return jnp.clip(values, -reach, reach).astype(kind)


def setup_inputs(seed: int = 0) -> dict:
    key_list = jax.random.split(jax.random.key(seed), 6)
    grads = scatter_about(key_list[0], (REPS, LOOP, P_SIZE), 1.0, 6.0, ((0, 8), (1, 4)))
    master = scatter_about(key_list[1], (REPS, P_SIZE), 1.0, 6.0, ((0, 8), (1, 4)), jnp.float32)
    moment_one = scatter_about(key_list[2], (REPS, P_SIZE), 0.03, 0.4375, ((0, 8), (1, 4)), jnp.float32)
    moment_two = jnp.clip(jnp.exp(math.log(0.01) - 4.6051702 * jax.random.uniform(key_list[3], (REPS, P_SIZE), jnp.float32) ** block_levels(key_list[3], (REPS, P_SIZE), ((0, 8), (1, 4)), -0.2, 0.2)), 0.0001, 0.01)
    step_index = jax.random.randint(key_list[4], (1,), 0, 1000).astype(jnp.int32)
    return {"grads": grads, "master": master, "moment_one": moment_one, "moment_two": moment_two, "step_index": step_index}


def reference(grads, master, moment_one, moment_two, step_index):
    total = jnp.zeros(master.shape, jnp.float32)
    for zidx in range(N_ZERO):
        total = total + grads[:, zidx, :].astype(jnp.float32)
    g = total / N_ZERO
    tstep = step_index[0]
    count = (tstep + 1).astype(jnp.float32)
    m_new = 0.9 * moment_one + 0.1 * g
    v_new = 0.999 * moment_two + 0.001 * g * g
    corr_one = 1.0 - jnp.power(jnp.float32(0.9), count)
    corr_two = 1.0 - jnp.power(jnp.float32(0.999), count)
    fresh = master - 0.02 * (m_new / corr_one / (jnp.sqrt(v_new / corr_two) + 1e-08) + 0.1 * master)
    nbits = N_REP.bit_length() - 1
    bit = tstep % nbits
    rows = jnp.arange(N_REP, dtype=jnp.int32)
    partner = jnp.bitwise_xor(rows, jnp.left_shift(jnp.int32(1), bit.astype(jnp.int32)))
    averaged = 0.5 * (fresh + fresh[partner])
    return (averaged, m_new, v_new, averaged.astype(jnp.bfloat16))
```

```python
import functools

import jax
import jax.numpy as jnp
from jax import lax
from jax.experimental import pallas as pl
from jax.experimental.pallas import tpu as pltpu
from jax.sharding import PartitionSpec as P

LANES = 128
CUTS = (3, 3, 2)
UNITS = 8
OUTER = ((0, 1), (3, 2))
MIDDLE = ((1, 2), (2, 1))
INNER = ((1, 0), (2, 3))
bf16 = jnp.bfloat16
f32 = jnp.float32
ANY = pl.BlockSpec(memory_space=pl.ANY)


def send(value, pairs):
    return lax.ppermute(value, "zero", list(pairs))


def swapped(value, apart):
    mask = 2**apart
    return lax.ppermute(value, "rep", [(r, r ^ mask) for r in range(lax.axis_size("rep"))])


def block_of(start, size):
    rows = 2048
    while start % rows or size % rows:
        rows //= 2
    return rows


def far(z, p):
    return jnp.where(z < 2, 3 - p, p)


def call(body, name, zero, grid, ins, specs, outs, out_specs, alias=(), after=(), cost=0):
    extra = [ANY] * len(after)
    count = len(specs)

    def kernel(zs, *refs):
        body(zs, *refs[:count], *refs[count + len(after) :])

    return pl.pallas_call(
        kernel,
        name=name,
        out_shape=outs,
        grid_spec=pltpu.PrefetchScalarGridSpec(
            num_scalar_prefetch=1,
            grid=grid,
            in_specs=list(specs) + extra,
            out_specs=out_specs,
        ),
        input_output_aliases={a + 1: b for a, b in alias},
        cost_estimate=pl.CostEstimate(flops=cost, bytes_accessed=cost, transcendentals=0),
    )(zero, *ins, *after)


def pack_outer(zs, g, o):
    o[0] = g[0].reshape(o.shape[1:])


def add_first(zs, r, g, o):
    own = g[0].astype(f32).reshape(o.shape[1:])
    o[0] = (r[0].astype(f32) + own).astype(bf16)


def adam_body(zs, g, re, rm, ri, m, v, w, sc, *rest):
    mo, vo, fr, fb = rest[-4:]
    shape = fr.shape
    total = g[0].astype(f32).reshape(shape)
    total = total + re[0].astype(f32) + rm[0].astype(f32) + ri[0].astype(f32)
    grad = total * 0.25
    m_new = 0.9 * m[...].reshape(shape) + 0.1 * grad
    v_new = 0.999 * v[...].reshape(shape) + 0.001 * grad * grad
    mo[...] = m_new.reshape(mo.shape)
    vo[...] = v_new.reshape(vo.shape)
    old = w[...].reshape(shape)
    root = jnp.sqrt(v_new * sc[1]) + 1e-08
    fresh = old - 0.02 * (m_new * sc[0] / root + 0.1 * old)
    fr[...] = fresh
    fb[...] = fresh.astype(bf16)


def mean_body(zs, fr, *rest):
    nbits = len(rest) - 2 if len(rest) < 6 else len(rest) - 3
    others = rest[:nbits]
    wo, ab = rest[-2:]
    bit = zs[1]
    for level in range(nbits):

        @pl.when(bit == level)
        def _(level=level):
            avg = 0.5 * (fr[...] + others[level][...].astype(f32))
            wo[...] = avg.reshape(wo.shape)
            ab[...] = avg.astype(bf16)


def spread_body(zs, own, *rest):
    near, ends, o = rest[:3], rest[3:6], rest[-1]
    slot = pl.program_id(0)
    z = zs[0]
    inner = (z == 1) | (z == 2)

    @pl.when(slot == 0)
    def _():
        o[...] = own[...].reshape(o.shape)

    for k in range(3):

        @pl.when((slot == k + 1) & inner)
        def _(k=k):
            o[...] = near[k][...].reshape(o.shape)

        @pl.when((slot == k + 1) & ~inner)
        def _(k=k):
            o[...] = ends[k][...].reshape(o.shape)


def slot_shard(z, slot):
    inner = jnp.where(
        z == 1,
        jnp.where(slot == 1, 0, slot),
        jnp.where(slot == 1, 3, 3 - slot),
    )
    end = jnp.where(z == 0, slot, 3 - slot)
    other = jnp.where((z == 1) | (z == 2), inner, end)
    return jnp.where(slot == 0, z, other)


def line_step(grads, master, moment_one, moment_two, step_index):
    size = master.shape[1]
    rows = size // LANES
    nbits = lax.axis_size("rep").bit_length() - 1
    z = lax.axis_index("zero").astype(jnp.int32)
    tstep = step_index[0]
    count = (tstep + 1).astype(f32)
    scale = jnp.stack(
        [
            1.0 / (1.0 - jnp.power(f32(0.9), count)),
            1.0 / (1.0 - jnp.power(f32(0.999), count)),
        ]
    )
    scalars = jnp.stack([z, tstep % nbits])
    unit = rows // UNITS
    m_all = v_all = w_all = p_all = None
    start = 0
    packs, parts = [], []
    for cut in CUTS:
        n = cut * unit
        R = block_of(start, n)
        parts.append((start, n, R))
        start += n

    def grad_spec(index, R):
        return pl.BlockSpec((1, 1, R * LANES), index)

    def chunk_kernels(start, n, R):
        nb, base, per = n // R, start // R, rows // R
        row = lambda f: pl.BlockSpec((R, LANES), f)
        lead = lambda f: pl.BlockSpec((1, R, LANES), f)
        flat = pl.BlockSpec((1, R * LANES), lambda i, zs: (0, base + i))
        return nb, base, per, row, lead, flat

    def outer(part, after):
        start, n, R = part
        nb, base, per, row, lead, flat = chunk_kernels(*part)
        packed = call(
            pack_outer, "pack_outer", scalars, (3, nb), (grads,),
            [grad_spec(lambda p, i, zs: (0, 0, far(zs[0], p) * per + base + i), R)],
            jax.ShapeDtypeStruct((3, n, LANES), bf16),
            lead(lambda p, i, zs: (p, i, 0)), after=after, cost=3 * n * LANES * 6,
        )
        return send(packed, OUTER)

    def reduce_rest(part, r_out):
        start, n, R = part
        nb, base, per, row, lead, flat = chunk_kernels(*part)
        summed = call(
            add_first, "sum_middle", scalars, (2, nb), (r_out, grads),
            [lead(lambda p, i, zs: (p, i, 0)),
             grad_spec(lambda p, i, zs: (0, 0, far(zs[0], p) * per + base + i), R)],
            jax.ShapeDtypeStruct((2, n, LANES), bf16),
            lead(lambda p, i, zs: (p, i, 0)), cost=2 * n * LANES * 8,
        )
        r_mid = send(summed, MIDDLE)
        last = call(
            add_first, "sum_inner", scalars, (1, nb), (r_mid, grads),
            [lead(lambda p, i, zs: (0, i, 0)),
             grad_spec(lambda p, i, zs: (0, 0, far(zs[0], 3) * per + base + i), R)],
            jax.ShapeDtypeStruct((1, n, LANES), bf16),
            lead(lambda p, i, zs: (0, i, 0)), cost=n * LANES * 8,
        )
        r_in = send(last, INNER)
        return r_mid, r_in

    def adam(part, r_out, r_mid, r_in):
        nonlocal m_all, v_all
        start, n, R = part
        nb, base, per, row, lead, flat = chunk_kernels(*part)
        whole = jax.ShapeDtypeStruct((1, size), f32)
        ins = [grads, r_out, r_mid, r_in, moment_one, moment_two, master, scale]
        specs = [
            grad_spec(lambda i, zs: (0, 0, zs[0] * per + base + i), R),
            lead(lambda i, zs: (2, i, 0)),
            lead(lambda i, zs: (1, i, 0)),
            lead(lambda i, zs: (0, i, 0)),
            flat, flat, flat,
            pl.BlockSpec(memory_space=pltpu.SMEM),
        ]
        alias = ()
        if m_all is not None:
            alias = ((len(ins), 0), (len(ins) + 1, 1))
            ins += [m_all, v_all]
            specs += [ANY, ANY]
        m_all, v_all, fresh, fresh16 = call(
            adam_body, "adam", scalars, (nb,), ins, specs,
            (whole, whole, jax.ShapeDtypeStruct((n, LANES), f32),
             jax.ShapeDtypeStruct((n, LANES), bf16)),
            (flat, flat, row(lambda i, zs: (i, 0)), row(lambda i, zs: (i, 0))),
            alias=alias, cost=n * LANES * 40,
        )
        return fresh, fresh16

    def mean(part, fresh, others):
        nonlocal w_all
        start, n, R = part
        nb, base, per, row, lead, flat = chunk_kernels(*part)
        ins = [fresh, *others]
        pick = lambda level: row(lambda i, zs: (jnp.where(zs[1] == level, i, 0), 0))
        specs = [row(lambda i, zs: (i, 0))] + [pick(k) for k in range(len(others))]
        alias = ()
        if w_all is not None:
            alias = ((len(ins), 0),)
            ins.append(w_all)
            specs.append(ANY)
        body = functools.partial(mean_wrap, len(others))
        w_all, avg = call(
            body, "mean", scalars, (nb,), ins, specs,
            (jax.ShapeDtypeStruct((1, size), f32), jax.ShapeDtypeStruct((n, LANES), bf16)),
            (flat, row(lambda i, zs: (i, 0))), alias=alias, cost=n * LANES * 14,
        )
        return avg

    def spread(part, avg):
        nonlocal p_all
        start, n, R = part
        nb, base, per, row, lead, flat = chunk_kernels(*part)
        c1 = send(avg, OUTER)
        m1 = send(avg, MIDDLE)
        a1 = send(avg, INNER)
        m2 = send(c1, MIDDLE)
        a2 = send(m1, INNER)
        a3 = send(m2, INNER)
        ins = [avg, c1, m1, m2, a1, a2, a3]
        inner = lambda zs: (zs[0] == 1) | (zs[0] == 2)
        specs = [row(lambda s, i, zs: (jnp.where(s == 0, i, 0), 0))]
        for k in range(3):
            specs.append(row(lambda s, i, zs, k=k: (jnp.where((s == k + 1) & inner(zs), i, 0), 0)))
        for k in range(3):
            specs.append(row(lambda s, i, zs, k=k: (jnp.where((s == k + 1) & ~inner(zs), i, 0), 0)))
        alias = ()
        if p_all is not None:
            alias = ((len(ins), 0),)
            ins.append(p_all)
            specs.append(ANY)
        per4 = per
        p_all = call(
            spread_body, "spread", scalars, (4, nb), ins, specs,
            jax.ShapeDtypeStruct((1, 4 * size), bf16),
            pl.BlockSpec((1, R * LANES), lambda s, i, zs: (0, slot_shard(zs[0], s) * per4 + base + i)),
            alias=alias, cost=4 * n * LANES * 6,
        )

    received = []
    after = ()
    for k, part in enumerate(parts):
        received.append(outer(part, after))
    for k, part in enumerate(parts):
        r_mid, r_in = reduce_rest(part, received[k])
        fresh, fresh16 = adam(part, received[k], r_mid, r_in)
        others = [swapped(fresh16, level) for level in range(nbits)]
        avg = mean(part, fresh, others)
        spread(part, avg)
    return (w_all, m_all, v_all, p_all)


def mean_wrap(nbits, zs, fr, *rest):
    others = rest[:nbits]
    wo, ab = rest[-2:]
    for level in range(nbits):

        @pl.when(zs[1] == level)
        def _(level=level):
            avg = 0.5 * (fr[...] + others[level][...].astype(f32))
            wo[...] = avg.reshape(wo.shape)
            ab[...] = avg.astype(bf16)


def plain_step(grads, master, moment_one, moment_two, step_index):
    loop_size = lax.axis_size("zero")
    nbits = lax.axis_size("rep").bit_length() - 1
    tstep = step_index[0]
    count = (tstep + 1).astype(f32)
    terms = grads.reshape(-1, LANES)
    g = lax.psum_scatter(terms, "zero", scatter_dimension=0, tiled=True).astype(f32)
    g = g.reshape(master.shape) / loop_size
    m_new = 0.9 * moment_one + 0.1 * g
    v_new = 0.999 * moment_two + 0.001 * g * g
    corr_one = 1.0 - jnp.power(f32(0.9), count)
    corr_two = 1.0 - jnp.power(f32(0.999), count)
    fresh = master - 0.02 * (m_new / corr_one / (jnp.sqrt(v_new / corr_two) + 1e-08) + 0.1 * master)
    other = jnp.zeros_like(fresh)
    for level in range(nbits):
        other = jnp.where(tstep % nbits == level, swapped(fresh, level), other)
    averaged = 0.5 * (fresh + other)
    whole = lax.all_gather(averaged.astype(bf16).reshape(-1, LANES), "zero", axis=0, tiled=True)
    return (averaged, m_new, v_new, whole.reshape(1, -1))


def shards(*args):
    if lax.axis_size("zero") == 4:
        return line_step(*args)
    return plain_step(*args)


def solution(mesh):
    return jax.shard_map(
        shards,
        mesh=mesh,
        in_specs=(
            P("rep", "zero", None),
            P("rep", "zero"),
            P("rep", "zero"),
            P("rep", "zero"),
            P(),
        ),
        out_specs=(P("rep", "zero"), P("rep", "zero"), P("rep", "zero"), P("rep", None)),
        check_vma=False,
    )
```

```python
import functools

import jax
import jax.numpy as jnp
from jax import lax
from jax.experimental import pallas as pl
from jax.experimental.pallas import tpu as pltpu
from jax.sharding import PartitionSpec as P


LANES = 128
VMEM = 67043328
CUTS = (3, 3, 2)
UNITS = 8
OUTER = ((0, 1), (3, 2))
MIDDLE = ((1, 2), (2, 1))
INNER = ((1, 0), (2, 3))
bf16 = jnp.bfloat16
f32 = jnp.float32
ANY = pl.BlockSpec(memory_space=pl.ANY)


def swapped(value, level):
    pairs = [(r, r ^ 2**level) for r in range(lax.axis_size("rep"))]
    return lax.ppermute(value, "rep", pairs)


def crossed(value, mask):
    return lax.ppermute(value, "zero", [(i, i ^ mask) for i in range(lax.axis_size("zero"))])


def block_of(start, size, most):
    rows = 1
    while rows < most and not (start % (2 * rows) or size % (2 * rows)):
        rows *= 2
    return rows


def far(z, p):
    return jnp.where(z < 2, 3 - p, p)


def pieces(rows, most):
    step = block_of(0, rows, most)

    def run(body):
        def one(i, carry):
            at = pl.multiple_of(i * step, step)
            flat = pl.ds(pl.multiple_of(i * (step * LANES), step * LANES), step * LANES)
            body(pl.ds(at, step), flat, step)
            return carry

        lax.fori_loop(0, rows // step, one, 0)

    return run


def call(body, scalars, grid, ins, specs, outs, out_specs, alias=(), cost=0):
    return pl.pallas_call(
        body,
        out_shape=outs,
        grid_spec=pltpu.PrefetchScalarGridSpec(
            num_scalar_prefetch=1, grid=grid, in_specs=list(specs), out_specs=out_specs
        ),
        input_output_aliases={a + 1: b for a, b in alias},
        cost_estimate=pl.CostEstimate(flops=cost, bytes_accessed=cost, transcendentals=0),
        compiler_params=pltpu.CompilerParams(vmem_limit_bytes=VMEM),
    )(scalars, *ins)


def pack_body(zs, *refs):
    half = len(refs) // 2
    rows = refs[half].shape[0]

    @pieces(rows, 256)
    def _(row, flat, step):
        for g, o in zip(refs[:half], refs[half:]):
            o[row, :] = g[0, :, flat].reshape(step, LANES)


def sum_body(zs, *refs):
    count = len(refs) // 3
    rows = refs[-1].shape[0]

    @pieces(rows, 128)
    def _(row, flat, step):
        for k in range(count):
            r, g, o = refs[2 * k], refs[2 * k + 1], refs[2 * count + k]
            own = g[0, :, flat].astype(f32).reshape(step, LANES)
            o[row, :] = (r[row, :].astype(f32) + own).astype(bf16)


def adam_body(zs, g, ra, rb, rc, m, v, w, sc, *rest):
    mo, vo, fr, fb = rest[-4:]
    one, two = sc[0], sc[1]

    @pieces(fr.shape[0], 64)
    def _(row, flat, step):
        shape = (step, LANES)
        total = g[0, :, flat].astype(f32).reshape(shape)
        total = total + ra[row, :].astype(f32) + rb[row, :].astype(f32) + rc[row, :].astype(f32)
        grad = total * 0.25
        m_new = 0.9 * m[:, flat].reshape(shape) + 0.1 * grad
        v_new = 0.999 * v[:, flat].reshape(shape) + 0.001 * grad * grad
        mo[:, flat] = m_new.reshape(1, step * LANES)
        vo[:, flat] = v_new.reshape(1, step * LANES)
        old = w[:, flat].reshape(shape)
        root = jnp.sqrt(v_new * two) + 1e-08
        fresh = old - 0.02 * (m_new * one / root + 0.1 * old)
        fr[row, :] = fresh
        fb[row, :] = fresh.astype(bf16)


def mean_body(zs, fr, other, *rest):
    wo, mine, yours = rest[-3:]

    def write(to):
        @pieces(fr.shape[0], 64)
        def _(row, flat, step):
            avg = 0.5 * (fr[row, :] + other[row, :].astype(f32))
            wo[:, flat] = avg.reshape(1, step * LANES)
            to[row, :] = avg.astype(bf16)

    pl.when(pl.program_id(0) == 0)(lambda: write(mine))
    pl.when(pl.program_id(0) == 1)(lambda: write(yours))


def spread_body(zs, *refs):
    o = refs[-1]
    place = pl.program_id(0)

    for k in range(8):

        @pl.when(place == k)
        def _(src=refs[k]):
            @pieces(src.shape[0], 256)
            def _(row, flat, step):
                o[:, flat] = src[row, :].reshape(1, step * LANES)


def line_branch(level, grads, master, moment_one, moment_two, step_index):
    size = master.shape[1]
    rows = size // LANES
    z = lax.axis_index("zero").astype(jnp.int32)
    half = (lax.axis_index("rep").astype(jnp.int32) // 2**level) % 2
    count = (step_index[0] + 1).astype(f32)
    scale = jnp.stack(
        [1.0 / (1.0 - jnp.power(f32(0.9), count)), 1.0 / (1.0 - jnp.power(f32(0.999), count))]
    )
    scalars = jnp.stack([z, half])
    unit = rows // UNITS
    kept = {}
    whole = jax.ShapeDtypeStruct((1, size), f32)
    compact = lambda n: jax.ShapeDtypeStruct((n, LANES), bf16)

    def plan(part, most=2048):
        _, start, n = part
        R = block_of(start, n, most)
        return R, n // R, start // R, rows // R

    row_of = lambda R, f: pl.BlockSpec((R, LANES), f)
    grad_of = lambda R, f: pl.BlockSpec((1, 1, R * LANES), f)
    flat_of = lambda R, f: pl.BlockSpec((1, R * LANES), f)

    def own_grad(R, per, base, p):
        return grad_of(R, lambda i, zs: (0, 0, far(zs[0], p) * per + base + i))

    def pack(part, places):
        _, _, n = part
        R, nb, base, per = plan(part, 1024)
        return call(
            pack_body, scalars, (nb,), [grads] * len(places),
            [own_grad(R, per, base, p) for p in places],
            [compact(n)] * len(places),
            [row_of(R, lambda i, zs: (i, 0))] * len(places),
            cost=n * LANES * 6 * len(places),
        )

    def add(part, received, places):
        _, _, n = part
        R, nb, base, per = plan(part, 1024)
        ins, specs = [], []
        for r, p in zip(received, places):
            ins += [r, grads]
            specs += [row_of(R, lambda i, zs: (i, 0)), own_grad(R, per, base, p)]
        return call(
            sum_body, scalars, (nb,), ins, specs,
            [compact(n)] * len(places),
            [row_of(R, lambda i, zs: (i, 0))] * len(places),
            cost=n * LANES * 8 * len(places),
        )

    def send(value, pairs):
        return lax.ppermute(value, "zero", list(pairs))

    def keep(names, ins, specs, first):
        if names[0] not in kept:
            return ()
        alias = tuple((len(ins) + i, first + i) for i in range(len(names)))
        ins += [kept[name] for name in names]
        specs += [ANY] * len(names)
        return alias

    def adam(part, received):
        _, _, n = part
        R, nb, base, per = plan(part, 1024)
        row = row_of(R, lambda i, zs: (i, 0))
        flat = flat_of(R, lambda i, zs: (0, base + i))
        ins = [grads, *received, moment_one, moment_two, master, scale]
        specs = [grad_of(R, lambda i, zs: (0, 0, zs[0] * per + base + i)), row, row, row]
        specs += [flat, flat, flat, pl.BlockSpec(memory_space=pltpu.SMEM)]
        alias = keep(("m", "v"), ins, specs, 0)
        kept["m"], kept["v"], fresh, fresh16 = call(
            adam_body, scalars, (nb,), ins, specs,
            (whole, whole, jax.ShapeDtypeStruct((n, LANES), f32), compact(n)),
            (flat, flat, row, row), alias, cost=n * LANES * 40,
        )
        return fresh, fresh16

    def mean(part, fresh, other):
        _, start, n = part
        R = block_of(start, n // 2, 1024)
        nh, base = n // 2 // R, start // R
        at = lambda p, i, zs: jnp.where(p == 0, zs[1], 1 - zs[1]) * nh + i
        row = row_of(R, lambda p, i, zs: (at(p, i, zs), 0))
        ins, specs = [fresh, other], [row, row]
        alias = keep(("w",), ins, specs, 0)
        hold = lambda first: row_of(
            R, lambda p, i, zs: (jnp.clip((p - first) * nh + i, 0, nh - 1), 0)
        )
        kept["w"], mine, yours = call(
            mean_body, scalars, (2, nh), ins, specs,
            (whole, compact(n // 2), compact(n // 2)),
            (flat_of(R, lambda p, i, zs: (0, base + at(p, i, zs))), hold(0), hold(1)),
            alias, cost=n * LANES * 14,
        )
        return mine, yours

    def spread(part, mine, yours):
        _, start, n = part
        R = block_of(start, n // 2, 1024)
        nh, base, per = n // 2 // R, start // R, rows // R
        ins = [mine, yours]
        for mask in (1, 2, 3):
            got = crossed(mine, mask)
            ins += [got, swapped(got, level)]
        specs = [
            row_of(R, lambda q, i, zs, at=at: (jnp.clip((q - at) * nh + i, 0, nh - 1), 0))
            for at in range(8)
        ]
        alias = keep(("p",), ins, specs, 0)

        def out(q, i, zs):
            shard = jnp.bitwise_xor(zs[0], q // 2)
            side = jnp.where(q % 2 == 0, zs[1], 1 - zs[1])
            return (0, shard * per + base + side * nh + i)

        kept["p"] = call(
            spread_body, scalars, (8, nh), ins, specs,
            jax.ShapeDtypeStruct((1, 4 * size), bf16), flat_of(R, out),
            alias, cost=n * LANES * 24,
        )

    parts, start = [], 0
    for k, cut in enumerate(CUTS):
        parts.append((k, start, cut * unit))
        start += cut * unit
    for part in parts:
        k = part[0]
        (e,) = pack(part, (0,))
        f, g = pack(part, (1, 2))
        re = send(e, OUTER)
        rf = send(f, OUTER)
        rg = send(g, OUTER)
        (sm,) = add(part, (re,), (0,))
        rm = send(sm, MIDDLE)
        sn, si = add(part, (rf, rm), (1, 3))
        rn = send(sn, MIDDLE)
        ri = send(si, INNER)
        fresh, fresh16 = adam(part, (rg, rn, ri))
        other = swapped(fresh16, level)
        mine, yours = mean(part, fresh, other)
        spread(part, mine, yours)
    return kept["w"], kept["m"], kept["v"], kept["p"]


def line_step(*args):
    nbits = lax.axis_size("rep").bit_length() - 1

    def branch(level, *args):
        return line_branch(level, *args)

    bit = args[-1][0] % nbits
    return lax.switch(bit, [functools.partial(branch, b) for b in range(nbits)], *args)


def plain_step(grads, master, moment_one, moment_two, step_index):
    loop_size = lax.axis_size("zero")
    nbits = lax.axis_size("rep").bit_length() - 1
    tstep = step_index[0]
    count = (tstep + 1).astype(f32)
    terms = grads.reshape(-1, LANES)
    g = lax.psum_scatter(terms, "zero", scatter_dimension=0, tiled=True).astype(f32)
    g = g.reshape(master.shape) / loop_size
    m_new = 0.9 * moment_one + 0.1 * g
    v_new = 0.999 * moment_two + 0.001 * g * g
    corr_one = 1.0 - jnp.power(f32(0.9), count)
    corr_two = 1.0 - jnp.power(f32(0.999), count)
    fresh = master - 0.02 * (m_new / corr_one / (jnp.sqrt(v_new / corr_two) + 1e-08) + 0.1 * master)
    other = jnp.zeros_like(fresh)
    for level in range(nbits):
        other = jnp.where(tstep % nbits == level, swapped(fresh, level), other)
    averaged = 0.5 * (fresh + other)
    whole = lax.all_gather(averaged.astype(bf16).reshape(-1, LANES), "zero", axis=0, tiled=True)
    return (averaged, m_new, v_new, whole.reshape(1, -1))


def shards(*args):
    if lax.axis_size("zero") == 4:
        return line_step(*args)
    return plain_step(*args)


def solution(mesh):
    return jax.shard_map(
        shards,
        mesh=mesh,
        in_specs=(
            P("rep", "zero", None),
            P("rep", "zero"),
            P("rep", "zero"),
            P("rep", "zero"),
            P(),
        ),
        out_specs=(P("rep", "zero"), P("rep", "zero"), P("rep", "zero"), P("rep", None)),
        check_vma=False,
    )
```

```python
import functools

import jax
import jax.numpy as jnp
from jax import lax
from jax.experimental import pallas as pl
from jax.experimental.pallas import tpu as pltpu
from jax.sharding import PartitionSpec as P


LANES = 128
VMEM = 67043328
CUTS = (3, 3, 2)
UNITS = 8
OUTER = ((0, 1), (3, 2))
MIDDLE = ((1, 2), (2, 1))
INNER = ((1, 0), (2, 3))
bf16 = jnp.bfloat16
f32 = jnp.float32
ANY = pl.BlockSpec(memory_space=pl.ANY)


def swapped(value, level):
    pairs = [(r, r ^ 2**level) for r in range(lax.axis_size("rep"))]
    return lax.ppermute(value, "rep", pairs)


def crossed(value, mask):
    return lax.ppermute(value, "zero", [(i, i ^ mask) for i in range(lax.axis_size("zero"))])


def far(z, p):
    return jnp.where(z < 2, 3 - p, p)


def pieces(rows, most):
    step = most
    while rows % step:
        step //= 2

    def run(body):
        def one(i, carry):
            at = pl.multiple_of(i * step, step)
            flat = pl.ds(pl.multiple_of(i * (step * LANES), step * LANES), step * LANES)
            body(pl.ds(at, step), flat, step)
            return carry

        lax.fori_loop(0, rows // step, one, 0)

    return run


def pack_body(sc, reads, writes):
    (g,), (o,) = reads, writes

    @pieces(o.shape[0], 256)
    def _(row, flat, step):
        o[row, :] = g[0, :, flat].reshape(step, LANES)


def sum_body(sc, reads, writes):
    (r, g), (o,) = reads, writes

    @pieces(o.shape[0], 128)
    def _(row, flat, step):
        own = g[0, :, flat].astype(f32).reshape(step, LANES)
        o[row, :] = (r[row, :].astype(f32) + own).astype(bf16)


def adam_body(sc, reads, writes):
    g, ra, rb, rc, m, v, w = reads
    mo, vo, fr, fb = writes
    one, two = sc[0], sc[1]

    @pieces(fr.shape[0], 64)
    def _(row, flat, step):
        shape = (step, LANES)
        total = g[0, :, flat].astype(f32).reshape(shape)
        total = total + ra[row, :].astype(f32) + rb[row, :].astype(f32) + rc[row, :].astype(f32)
        grad = total * 0.25
        m_new = 0.9 * m[:, flat].reshape(shape) + 0.1 * grad
        v_new = 0.999 * v[:, flat].reshape(shape) + 0.001 * grad * grad
        mo[:, flat] = m_new.reshape(1, step * LANES)
        vo[:, flat] = v_new.reshape(1, step * LANES)
        old = w[:, flat].reshape(shape)
        root = jnp.sqrt(v_new * two) + 1e-08
        fresh = old - 0.02 * (m_new * one / root + 0.1 * old)
        fr[row, :] = fresh
        fb[row, :] = fresh.astype(bf16)


def mean_body(sc, reads, writes):
    (fr, other), (wo, ab) = reads, writes

    @pieces(fr.shape[0], 64)
    def _(row, flat, step):
        avg = 0.5 * (fr[row, :] + other[row, :].astype(f32))
        wo[:, flat] = avg.reshape(1, step * LANES)
        ab[row, :] = avg.astype(bf16)


def spread_body(sc, reads, writes):
    (src,), (o,) = reads, writes

    @pieces(src.shape[0], 256)
    def _(row, flat, step):
        o[:, flat] = src[row, :].reshape(1, step * LANES)


def staged(body, scalars, ins, outs, plan, alias=(), scale=None, cost=0):
    count = len(ins)
    buffers = [(shape, kind) for reads, writes in plan for _, _, shape, kind in reads + writes]

    def kernel(zs, *refs):
        if scale is not None:
            sc, refs = refs[0], refs[1:]
        else:
            sc = None
        sources, sinks = refs[:count], refs[count : count + len(outs)]
        scratch, sems = refs[count + len(outs) : -1], refs[-1]
        at, work = 0, []
        for reads, writes in plan:
            loads, stores = [], []
            for i, where, _, _ in reads:
                copy = pltpu.make_async_copy(sources[i].at[where(zs)], scratch[at], sems.at[at])
                loads.append((copy, scratch[at]))
                at += 1
            for i, where, _, _ in writes:
                copy = pltpu.make_async_copy(scratch[at], sinks[i].at[where(zs)], sems.at[at])
                stores.append((copy, scratch[at]))
                at += 1
            work.append((loads, stores))
        for loads, _ in work:
            for copy, _ in loads:
                copy.start()
        for loads, stores in work:
            for copy, _ in loads:
                copy.wait()
            body(sc, [ref for _, ref in loads], [ref for _, ref in stores])
            for copy, _ in stores:
                copy.start()
        for _, stores in work:
            for copy, _ in stores:
                copy.wait()

    first = [] if scale is None else [scale]
    shift = 1 + len(first)
    return pl.pallas_call(
        kernel,
        out_shape=outs,
        grid_spec=pltpu.PrefetchScalarGridSpec(
            num_scalar_prefetch=1,
            grid=(),
            in_specs=[pl.BlockSpec(memory_space=pltpu.SMEM)] * len(first) + [ANY] * count,
            out_specs=[ANY] * len(outs),
            scratch_shapes=[pltpu.VMEM(shape, kind) for shape, kind in buffers]
            + [pltpu.SemaphoreType.DMA((len(buffers),))],
        ),
        input_output_aliases={a + shift: b for a, b in alias},
        cost_estimate=pl.CostEstimate(flops=cost, bytes_accessed=cost, transcendentals=0),
        compiler_params=pltpu.CompilerParams(vmem_limit_bytes=VMEM),
    )(scalars, *first, *ins)


def line_branch(level, grads, master, moment_one, moment_two, step_index):
    size = master.shape[1]
    rows = size // LANES
    z = lax.axis_index("zero").astype(jnp.int32)
    half = (lax.axis_index("rep").astype(jnp.int32) // 2**level) % 2
    count = (step_index[0] + 1).astype(f32)
    scale = jnp.stack(
        [1.0 / (1.0 - jnp.power(f32(0.9), count)), 1.0 / (1.0 - jnp.power(f32(0.999), count))]
    )
    scalars = jnp.stack([z, half])
    unit = rows // UNITS
    kept = {}
    whole = jax.ShapeDtypeStruct((1, size), f32)
    compact = lambda n: jax.ShapeDtypeStruct((n, LANES), bf16)

    def cuts(n, most):
        parts = max(1, n // most)
        return [(i * (n // parts), n // parts) for i in range(parts)]

    def rows_at(i, at, n, kind=bf16):
        return (i, lambda zs: pl.ds(at, n), (n, LANES), kind)

    def flat_at(i, at, n):
        return (i, lambda zs: (slice(None), pl.ds(at * LANES, n * LANES)), (1, n * LANES), f32)

    def grad_at(i, shard, at, n):
        def where(zs):
            first = pl.multiple_of((shard(zs[0]) * rows + at) * LANES, 8 * LANES)
            return (slice(None), slice(None), pl.ds(first, n * LANES))

        return (i, where, (1, 1, n * LANES), bf16)

    def pack(part, places):
        _, start, n = part
        plan = [
            ([grad_at(0, functools.partial(far, p=p), start + at, r)], [rows_at(q, at, r)])
            for q, p in enumerate(places)
            for at, r in cuts(n, 1024)
        ]
        return staged(
            pack_body, scalars, [grads], [compact(n)] * len(places), plan,
            cost=n * LANES * 6 * len(places),
        )

    def add(part, received, places):
        _, start, n = part
        plan = [
            (
                [rows_at(1 + q, at, r), grad_at(0, functools.partial(far, p=p), start + at, r)],
                [rows_at(q, at, r)],
            )
            for q, p in enumerate(places)
            for at, r in cuts(n, 1024)
        ]
        return staged(
            sum_body, scalars, [grads, *received], [compact(n)] * len(places), plan,
            cost=n * LANES * 8 * len(places),
        )

    def send(value, pairs):
        return lax.ppermute(value, "zero", list(pairs))

    def keep(names, ins):
        if names[0] not in kept:
            return ()
        ins += [kept[name] for name in names]
        return tuple((len(ins) - len(names) + i, i) for i in range(len(names)))

    def adam(part, received):
        _, start, n = part
        ins = [grads, *received, moment_one, moment_two, master]
        alias = keep(("m", "v"), ins)
        plan = [
            (
                [grad_at(0, lambda z: z, start + at, r)]
                + [rows_at(i, at, r) for i in (1, 2, 3)]
                + [flat_at(i, start + at, r) for i in (4, 5, 6)],
                [flat_at(0, start + at, r), flat_at(1, start + at, r)]
                + [rows_at(2, at, r, f32), rows_at(3, at, r)],
            )
            for at, r in cuts(n, 512)
        ]
        kept["m"], kept["v"], fresh, fresh16 = staged(
            adam_body, scalars, ins,
            [whole, whole, jax.ShapeDtypeStruct((n, LANES), f32), compact(n)],
            plan, alias, scale, cost=n * LANES * 40,
        )
        return fresh, fresh16

    def side(zs, p):
        return zs[1] if p == 0 else 1 - zs[1]

    def mean(part, fresh, other):
        _, start, n = part
        ins = [fresh, other]
        alias = keep(("w",), ins)
        plan = []
        for p in (0, 1):
            for at, r in cuts(n // 2, 512):
                row = lambda zs, p=p, at=at: pl.multiple_of(side(zs, p) * (n // 2) + at, 8)
                here = lambda zs, row=row, r=r: pl.ds(row(zs), r)
                flat = lambda zs, row=row, r=r: (
                    slice(None),
                    pl.ds(pl.multiple_of((start + row(zs)) * LANES, 8 * LANES), r * LANES),
                )
                plan.append(
                    (
                        [(0, here, (r, LANES), f32), (1, here, (r, LANES), bf16)],
                        [(0, flat, (1, r * LANES), f32), rows_at(1 + p, at, r)],
                    )
                )
        kept["w"], mine, yours = staged(
            mean_body, scalars, ins, [whole, compact(n // 2), compact(n // 2)],
            plan, alias, cost=n * LANES * 14,
        )
        return mine, yours

    def spread(part, mine, yours):
        _, start, n = part
        nh = n // 2
        ins = [mine, yours]
        for mask in (1, 2, 3):
            got = crossed(mine, mask)
            ins += [got, swapped(got, level)]
        plan = []
        for q in range(8):

            def where(zs, q=q):
                shard = jnp.bitwise_xor(zs[0], q // 2)
                first = shard * rows + start + side(zs, q % 2) * nh
                return (slice(None), pl.ds(pl.multiple_of(first * LANES, 8 * LANES), nh * LANES))

            plan.append(([rows_at(q, 0, nh)], [(0, where, (1, nh * LANES), bf16)]))
        alias = keep(("p",), ins)
        (kept["p"],) = staged(
            spread_body, scalars, ins,
            [jax.ShapeDtypeStruct((1, 4 * size), bf16)], plan, alias, cost=n * LANES * 24,
        )

    parts, start = [], 0
    for k, cut in enumerate(CUTS):
        parts.append((k, start, cut * unit))
        start += cut * unit
    for part in parts:
        k = part[0]
        (e,) = pack(part, (0,))
        f, g = pack(part, (1, 2))
        re = send(e, OUTER)
        rf = send(f, OUTER)
        rg = send(g, OUTER)
        (sm,) = add(part, (re,), (0,))
        rm = send(sm, MIDDLE)
        sn, si = add(part, (rf, rm), (1, 3))
        rn = send(sn, MIDDLE)
        ri = send(si, INNER)
        fresh, fresh16 = adam(part, (rg, rn, ri))
        other = swapped(fresh16, level)
        mine, yours = mean(part, fresh, other)
        spread(part, mine, yours)
    return kept["w"], kept["m"], kept["v"], kept["p"]


def line_step(*args):
    nbits = lax.axis_size("rep").bit_length() - 1

    def branch(level, *args):
        return line_branch(level, *args)

    bit = args[-1][0] % nbits
    return lax.switch(bit, [functools.partial(branch, b) for b in range(nbits)], *args)


def plain_step(grads, master, moment_one, moment_two, step_index):
    loop_size = lax.axis_size("zero")
    nbits = lax.axis_size("rep").bit_length() - 1
    tstep = step_index[0]
    count = (tstep + 1).astype(f32)
    terms = grads.reshape(-1, LANES)
    g = lax.psum_scatter(terms, "zero", scatter_dimension=0, tiled=True).astype(f32)
    g = g.reshape(master.shape) / loop_size
    m_new = 0.9 * moment_one + 0.1 * g
    v_new = 0.999 * moment_two + 0.001 * g * g
    corr_one = 1.0 - jnp.power(f32(0.9), count)
    corr_two = 1.0 - jnp.power(f32(0.999), count)
    fresh = master - 0.02 * (m_new / corr_one / (jnp.sqrt(v_new / corr_two) + 1e-08) + 0.1 * master)
    other = jnp.zeros_like(fresh)
    for level in range(nbits):
        other = jnp.where(tstep % nbits == level, swapped(fresh, level), other)
    averaged = 0.5 * (fresh + other)
    whole = lax.all_gather(averaged.astype(bf16).reshape(-1, LANES), "zero", axis=0, tiled=True)
    return (averaged, m_new, v_new, whole.reshape(1, -1))


def shards(*args):
    if lax.axis_size("zero") == 4:
        return line_step(*args)
    return plain_step(*args)


def solution(mesh):
    return jax.shard_map(
        shards,
        mesh=mesh,
        in_specs=(
            P("rep", "zero", None),
            P("rep", "zero"),
            P("rep", "zero"),
            P("rep", "zero"),
            P(),
        ),
        out_specs=(P("rep", "zero"), P("rep", "zero"), P("rep", "zero"), P("rep", None)),
        check_vma=False,
    )
```

```python
import functools

import jax
import jax.numpy as jnp
from jax import lax
from jax.experimental import pallas as pl
from jax.experimental.pallas import tpu as pltpu
from jax.sharding import PartitionSpec as P


LANES = 128
VMEM = 67043328
CUTS = (5, 7, 4)
UNITS = 16
CHAIN = "ccd"
OUTER = ((0, 1), (3, 2))
MIDDLE = ((1, 2), (2, 1))
INNER = ((1, 0), (2, 3))
bf16 = jnp.bfloat16
f32 = jnp.float32
ANY = pl.BlockSpec(memory_space=pl.ANY)


def swapped(value, level):
    pairs = [(r, r ^ 2**level) for r in range(lax.axis_size("rep"))]
    return lax.ppermute(value, "rep", pairs)


def swapped_among(value, level, places):
    n = lax.axis_size("zero")
    pairs = [
        (r * n + i, (r ^ 2**level) * n + i) for r in range(lax.axis_size("rep")) for i in places
    ]
    return lax.ppermute(value, ("rep", "zero"), pairs)


def crossed(value, mask):
    return lax.ppermute(value, "zero", [(i, i ^ mask) for i in range(lax.axis_size("zero"))])


def far(z, p):
    return jnp.where(z < 2, 3 - p, p)


def pieces(rows, most):
    step = most
    while rows % step:
        step //= 2

    def run(body):
        def one(i, carry):
            at = pl.multiple_of(i * step, step)
            flat = pl.ds(pl.multiple_of(i * (step * LANES), step * LANES), step * LANES)
            body(pl.ds(at, step), flat, step)
            return carry

        lax.fori_loop(0, rows // step, one, 0)

    return run


def pack_body(sc, reads, writes):
    (g,), (o,) = reads, writes

    @pieces(o.shape[0], 64)
    def _(row, flat, step):
        o[row, :] = g[0, :, flat].reshape(step, LANES)


def sum_body(sc, reads, writes):
    (r, g), (o,) = reads, writes

    @pieces(o.shape[0], 64)
    def _(row, flat, step):
        own = g[0, :, flat].astype(f32).reshape(step, LANES)
        o[row, :] = (r[row, :].astype(f32) + own).astype(bf16)


def adam_body(sc, reads, writes):
    g, ra, rb, rc, m, v, w = reads
    mo, vo, fr, fb = writes
    one, two = sc[0], sc[1]

    @pieces(fr.shape[0], 64)
    def _(row, flat, step):
        shape = (step, LANES)
        total = g[0, :, flat].astype(f32).reshape(shape)
        total = total + ra[row, :].astype(f32) + rb[row, :].astype(f32) + rc[row, :].astype(f32)
        grad = total * 0.25
        m_new = 0.9 * m[:, flat].reshape(shape) + 0.1 * grad
        v_new = 0.999 * v[:, flat].reshape(shape) + 0.001 * grad * grad
        mo[:, flat] = m_new.reshape(1, step * LANES)
        vo[:, flat] = v_new.reshape(1, step * LANES)
        old = w[:, flat].reshape(shape)
        root = jnp.sqrt(v_new * two) + 1e-08
        fresh = old - 0.02 * (m_new * one / root + 0.1 * old)
        fr[row, :] = fresh
        fb[row, :] = fresh.astype(bf16)


def mean_body(sc, reads, writes):
    (fr, other), (wo, ab) = reads, writes

    @pieces(fr.shape[0], 64)
    def _(row, flat, step):
        avg = 0.5 * (fr[row, :] + other[row, :].astype(f32))
        wo[:, flat] = avg.reshape(1, step * LANES)
        ab[row, :] = avg.astype(bf16)


def spread_body(sc, reads, writes):
    (src,), (o,) = reads, writes

    @pieces(src.shape[0], 64)
    def _(row, flat, step):
        o[:, flat] = src[row, :].reshape(1, step * LANES)


def staged(body, scalars, ins, outs, plan, alias=(), scale=None, cost=0):
    count = len(ins)
    buffers = [(shape, kind) for reads, writes in plan for _, _, shape, kind, *_ in reads + writes]

    def kernel(zs, *refs):
        if scale is not None:
            sc, refs = refs[0], refs[1:]
        else:
            sc = None
        sources, sinks = refs[:count], refs[count : count + len(outs)]
        scratch, sems = refs[count + len(outs) : -1], refs[-1]
        at, work = 0, []
        for reads, writes in plan:
            loads, stores = [], []
            for i, where, _, _, *choice in reads:
                def load(i, at=at, where=where):
                    return pltpu.make_async_copy(sources[i].at[where(zs)], scratch[at], sems.at[at])

                loads.append((load, choice[0] if choice else (i, i), scratch[at]))
                at += 1
            for i, where, _, _ in writes:
                copy = pltpu.make_async_copy(scratch[at], sinks[i].at[where(zs)], sems.at[at])
                stores.append((copy, scratch[at]))
                at += 1
            work.append((loads, stores))
        middle = (zs[0] == 1) | (zs[0] == 2)
        for loads, _ in work:
            for load, (i, j), _ in loads:
                if i == j:
                    load(i).start()
                    continue
                pl.when(middle)(lambda load=load, i=i: load(i).start())
                pl.when(~middle)(lambda load=load, j=j: load(j).start())
        for loads, stores in work:
            for load, (i, _), _ in loads:
                load(i).wait()
            body(sc, [ref for _, _, ref in loads], [ref for _, ref in stores])
            for copy, _ in stores:
                copy.start()
        for _, stores in work:
            for copy, _ in stores:
                copy.wait()

    first = [] if scale is None else [scale]
    shift = 1 + len(first)
    return pl.pallas_call(
        kernel,
        out_shape=outs,
        grid_spec=pltpu.PrefetchScalarGridSpec(
            num_scalar_prefetch=1,
            grid=(),
            in_specs=[pl.BlockSpec(memory_space=pltpu.SMEM)] * len(first) + [ANY] * count,
            out_specs=[ANY] * len(outs),
            scratch_shapes=[pltpu.VMEM(shape, kind) for shape, kind in buffers]
            + [pltpu.SemaphoreType.DMA((len(buffers),))],
        ),
        input_output_aliases={a + shift: b for a, b in alias},
        cost_estimate=pl.CostEstimate(flops=cost, bytes_accessed=cost, transcendentals=0),
        compiler_params=pltpu.CompilerParams(vmem_limit_bytes=VMEM),
    )(scalars, *first, *ins)


def line_branch(level, grads, master, moment_one, moment_two, step_index):
    size = master.shape[1]
    rows = size // LANES
    z = lax.axis_index("zero").astype(jnp.int32)
    half = (lax.axis_index("rep").astype(jnp.int32) // 2**level) % 2
    count = (step_index[0] + 1).astype(f32)
    scale = jnp.stack(
        [1.0 / (1.0 - jnp.power(f32(0.9), count)), 1.0 / (1.0 - jnp.power(f32(0.999), count))]
    )
    scalars = jnp.stack([z, half])
    unit = rows // UNITS
    kept = {}
    whole = jax.ShapeDtypeStruct((1, size), f32)
    compact = lambda n: jax.ShapeDtypeStruct((n, LANES), bf16)

    def cuts(n, most):
        parts = max(1, n // most)
        while n % (64 * parts):
            parts += 1
        return [(i * (n // parts), n // parts) for i in range(parts)]

    def rows_at(i, at, n, kind=bf16):
        return (i, lambda zs: pl.ds(at, n), (n, LANES), kind)

    def flat_at(i, at, n):
        return (i, lambda zs: (slice(None), pl.ds(at * LANES, n * LANES)), (1, n * LANES), f32)

    def grad_at(i, shard, at, n):
        def where(zs):
            first = pl.multiple_of((shard(zs[0]) * rows + at) * LANES, 8 * LANES)
            return (slice(None), slice(None), pl.ds(first, n * LANES))

        return (i, where, (1, 1, n * LANES), bf16)

    def pack(part, places):
        _, start, n = part
        plan = [
            ([grad_at(0, functools.partial(far, p=p), start + at, r)], [rows_at(q, at, r)])
            for q, p in enumerate(places)
            for at, r in cuts(n, 1024)
        ]
        return staged(
            pack_body, scalars, [grads], [compact(n)] * len(places), plan,
            cost=n * LANES * 6 * len(places),
        )

    def add(part, received, places):
        _, start, n = part
        plan = [
            (
                [rows_at(1 + q, at, r), grad_at(0, functools.partial(far, p=p), start + at, r)],
                [rows_at(q, at, r)],
            )
            for q, p in enumerate(places)
            for at, r in cuts(n, 1024)
        ]
        return staged(
            sum_body, scalars, [grads, *received], [compact(n)] * len(places), plan,
            cost=n * LANES * 8 * len(places),
        )

    def send(value, pairs):
        return lax.ppermute(value, "zero", list(pairs))

    def keep(names, ins):
        if names[0] not in kept:
            return ()
        ins += [kept[name] for name in names]
        return tuple((len(ins) - len(names) + i, i) for i in range(len(names)))

    def adam(part, received):
        _, start, n = part
        ins = [grads, *received, moment_one, moment_two, master]
        alias = keep(("m", "v"), ins)
        plan = [
            (
                [grad_at(0, lambda z: z, start + at, r)]
                + [rows_at(i, at, r) for i in (1, 2, 3)]
                + [flat_at(i, start + at, r) for i in (4, 5, 6)],
                [flat_at(0, start + at, r), flat_at(1, start + at, r)]
                + [rows_at(2, at, r, f32), rows_at(3, at, r)],
            )
            for at, r in cuts(n, 1024)
        ]
        kept["m"], kept["v"], fresh, fresh16 = staged(
            adam_body, scalars, ins,
            [whole, whole, jax.ShapeDtypeStruct((n, LANES), f32), compact(n)],
            plan, alias, scale, cost=n * LANES * 40,
        )
        return fresh, fresh16

    def side(zs, p):
        return zs[1] if p == 0 else 1 - zs[1]

    def mean(part, fresh, other):
        _, start, n = part
        ins = [fresh, other]
        alias = keep(("w",), ins)
        plan = []
        for p in (0, 1):
            for at, r in cuts(n // 2, 768):
                row = lambda zs, p=p, at=at: pl.multiple_of(side(zs, p) * (n // 2) + at, 8)
                here = lambda zs, row=row, r=r: pl.ds(row(zs), r)
                flat = lambda zs, row=row, r=r: (
                    slice(None),
                    pl.ds(pl.multiple_of((start + row(zs)) * LANES, 8 * LANES), r * LANES),
                )
                plan.append(
                    (
                        [(0, here, (r, LANES), f32), (1, here, (r, LANES), bf16)],
                        [(0, flat, (1, r * LANES), f32), rows_at(1 + p, at, r)],
                    )
                )
        kept["w"], mine, yours = staged(
            mean_body, scalars, ins, [whole, compact(n // 2), compact(n // 2)],
            plan, alias, cost=n * LANES * 14,
        )
        return mine, yours

    def spread(part, mine, yours):
        k, start, n = part
        nh = n // 2
        ins, slots = [mine, yours], [(0, 1)]

        def swap_halves(got, among):
            return swapped_among(got, level, among)

        got = crossed(mine, 1)
        ins += [got, swap_halves(got, range(4))]
        slots.append((2, 3))
        if CHAIN[k] == "d":
            for mask in (2, 3):
                got = crossed(mine, mask)
                slots.append((len(ins), len(ins) + 1))
                ins += [got, swap_halves(got, range(4))]
        else:
            m1 = send(mine, MIDDLE)
            m2 = send(got, MIDDLE)
            a2 = send(m1, INNER)
            a3 = send(m2, INNER)
            for mid, end in ((m2, a2), (m1, a3)):
                slots.append(tuple((len(ins) + i, len(ins) + 2 + i) for i in (0, 1)))
                ins += [mid, swap_halves(mid, (1, 2))]
                ins += [end, swap_halves(end, (0, 3))]
        plan = []
        for q in range(8):

            def where(zs, q=q):
                shard = jnp.bitwise_xor(zs[0], q // 2)
                first = shard * rows + start + side(zs, q % 2) * nh
                return (slice(None), pl.ds(pl.multiple_of(first * LANES, 8 * LANES), nh * LANES))

            source = slots[q // 2][q % 2]
            read = rows_at(source[0] if isinstance(source, tuple) else source, 0, nh)
            plan.append(([read + ((source,) if isinstance(source, tuple) else ())],
                         [(0, where, (1, nh * LANES), bf16)]))
        alias = keep(("p",), ins)
        (kept["p"],) = staged(
            spread_body, scalars, ins,
            [jax.ShapeDtypeStruct((1, 4 * size), bf16)], plan, alias, cost=n * LANES * 24,
        )

    parts, start = [], 0
    for k, cut in enumerate(CUTS):
        parts.append((k, start, cut * unit))
        start += cut * unit
    for part in parts:
        k = part[0]
        (e,) = pack(part, (0,))
        f, g = pack(part, (1, 2))
        re = send(e, OUTER)
        rf = send(f, OUTER)
        rg = send(g, OUTER)
        (sm,) = add(part, (re,), (0,))
        rm = send(sm, MIDDLE)
        sn, si = add(part, (rf, rm), (1, 3))
        rn = send(sn, MIDDLE)
        ri = send(si, INNER)
        fresh, fresh16 = adam(part, (rg, rn, ri))
        other = swapped(fresh16, level)
        mine, yours = mean(part, fresh, other)
        spread(part, mine, yours)
    return kept["w"], kept["m"], kept["v"], kept["p"]


def line_step(*args):
    nbits = lax.axis_size("rep").bit_length() - 1

    def branch(level, *args):
        return line_branch(level, *args)

    bit = args[-1][0] % nbits
    return lax.switch(bit, [functools.partial(branch, b) for b in range(nbits)], *args)


def plain_step(grads, master, moment_one, moment_two, step_index):
    loop_size = lax.axis_size("zero")
    nbits = lax.axis_size("rep").bit_length() - 1
    tstep = step_index[0]
    count = (tstep + 1).astype(f32)
    terms = grads.reshape(-1, LANES)
    g = lax.psum_scatter(terms, "zero", scatter_dimension=0, tiled=True).astype(f32)
    g = g.reshape(master.shape) / loop_size
    m_new = 0.9 * moment_one + 0.1 * g
    v_new = 0.999 * moment_two + 0.001 * g * g
    corr_one = 1.0 - jnp.power(f32(0.9), count)
    corr_two = 1.0 - jnp.power(f32(0.999), count)
    fresh = master - 0.02 * (m_new / corr_one / (jnp.sqrt(v_new / corr_two) + 1e-08) + 0.1 * master)
    other = jnp.zeros_like(fresh)
    for level in range(nbits):
        other = jnp.where(tstep % nbits == level, swapped(fresh, level), other)
    averaged = 0.5 * (fresh + other)
    whole = lax.all_gather(averaged.astype(bf16).reshape(-1, LANES), "zero", axis=0, tiled=True)
    return (averaged, m_new, v_new, whole.reshape(1, -1))


def shards(*args):
    if lax.axis_size("zero") == 4:
        return line_step(*args)
    return plain_step(*args)


def solution(mesh):
    return jax.shard_map(
        shards,
        mesh=mesh,
        in_specs=(
            P("rep", "zero", None),
            P("rep", "zero"),
            P("rep", "zero"),
            P("rep", "zero"),
            P(),
        ),
        out_specs=(P("rep", "zero"), P("rep", "zero"), P("rep", "zero"), P("rep", None)),
        check_vma=False,
    )
```
